256 devices in a mesh: row: 32 (over z_hi, x, core), col: 8 (over y, z_lo).
Axes of the slice: x: 4, y: 4, z: 8 (z_hi: 4, z_lo: 2; z = z_hi * 2 + z_lo), core: 2. Of those that a mesh axis runs over, the one named last changes fastest.
Arguments:
- amplitudes: bfloat16 [512, 640000], P(('row', 'col')), may hold values from -6 to 6
- integrals: bfloat16 [2, 800, 640000], P(None, None, ('row', 'col')), may hold values from -0.0078125 to 0.0078125
Outputs:
- ladder: float32 [512, 2, 800], P(('row', 'col'))
The draws below stay inside these ranges and needn't reach their ends.
All inputs are finite; a program needn't handle non-finite values.
Results may differ from the reference program's by a relative error of at most 0.0003.
Values may be sent and summed in bfloat16 or wider, within the bound.
A program may use at most 64 MiB of HBM per device.

```python
import jax
import jax.numpy as jnp
from jax import lax

NV = 800
A_WIN = 2
PAIRS = 512


def levels(rng, shape, cuts, smallest, top_value):
    level, own = 1.0, jax.random.fold_in(rng, 6)
    for position, parts in cuts:
        heights = jnp.exp(jax.random.uniform(jax.random.fold_in(own, position), (parts,), jnp.float32, smallest / len(cuts), top_value / len(cuts)))
        level = level * jnp.repeat(heights, shape[position] // parts).reshape([-1 if axis == position else 1 for axis in range(len(shape))])
    return level


def normal_values(key, shape, scale, most, shards=(), kind=jnp.bfloat16):
    drawn = jax.random.normal(key, shape, jnp.float32) * scale
    if len(shards) > 0:
        drawn = levels(key, shape, shards, -0.22, 0.18) * drawn
    return jnp.clip(drawn, min=-most, max=most).astype(kind)


def setup_inputs(seed: int = 0) -> dict:
    streams_of = jax.random.split(jax.random.key(seed), 3)
    amplitudes = normal_values(streams_of[0], (PAIRS, NV * NV), 1.0, 6.0, ((0, 256),))
    integrals = normal_values(streams_of[1], (A_WIN, NV, NV * NV), (NV * NV) ** -0.5, 0.0078125, ((2, 256),))
    return {"amplitudes": amplitudes, "integrals": integrals}


def reference(amplitudes, integrals):
    ladder_slabs = []
    for window_index in range(A_WIN):
        ladder_slabs.append(lax.dot_general(amplitudes, integrals[window_index], (((1,), (1,)), ((), ())), preferred_element_type=jnp.float32))
    return jnp.stack(ladder_slabs, axis=1)
```

```python
import functools

import jax
import jax.numpy as jnp
from jax import lax
from jax.experimental import pallas as pl
from jax.experimental.pallas import tpu as pltpu
from jax.sharding import PartitionSpec as P

MESH = pl.DeviceIdType.MESH
LANES = 128
WIDTH = 2500
TILES = 21
ROWS = 1600
WIDE = 1664
PHASES = 4
SOURCES = 64
CHUNK = 256


def index(z, y, x, k):
    return (z // 2) * 64 + x * 16 + k * 8 + y * 2 + lax.rem(z, 2)


def place(device):
    return {"row": device // 8, "col": lax.rem(device, 8)}


def kernel(
    amps, ints, out, buf, stage, weights, product, pair_in, sums, plane_in, z_out, z_in,
    send20, send21, recv, go, own, load, pair_s, pair_r, plane_s, plane_r, z_s, z_r,
):
    row, col = lax.axis_index("row"), lax.axis_index("col")
    me = row * 8 + col
    z = (row // 8) * 2 + lax.rem(col, 2)
    x = lax.rem(row // 2, 4)
    k = lax.rem(row, 2)
    y = col // 2
    parity = lax.rem(x + y + z, 2)
    phase_me = 2 * k + parity
    xh = x // 2
    slot = ((xh * 4 + y) * 2 + lax.rem(x, 2)) * 4 + z // 2
    mate = index(z, y, x, 1 - k)

    def first_tile(e):
        return (e * WIDTH) // LANES

    def offset(e):
        return lax.rem(e * WIDTH, LANES)

    def remote(src, dst, ssem, rsem, device):
        return pltpu.make_async_remote_copy(src, dst, ssem, rsem, device_id=place(device), device_id_type=MESH)

    barrier = pltpu.get_barrier_semaphore()

    def greet(i, _):
        pl.semaphore_signal(barrier, inc=1, device_id=place(lax.rem(me + i, 256)), device_id_type=MESH)
        return 0

    lax.fori_loop(1, 256, greet, 0)
    shift = offset(me)
    short = shift <= 60
    load_ints = pltpu.make_async_copy(ints, stage, load)
    load_ints.start()

    @pl.when(short)
    def _():
        for p in range(PHASES):
            buf[p, TILES - 1] = jnp.zeros((SOURCES, 2, LANES), jnp.bfloat16)

    def own_copy(n):
        return pltpu.make_async_copy(amps.at[pl.ds(first_tile(me), n)], buf.at[phase_me, pl.ds(0, n), slot], own)

    @pl.when(short)
    def _():
        own_copy(TILES - 1).start()

    @pl.when(jnp.logical_not(short))
    def _():
        own_copy(TILES).start()

    pl.semaphore_wait(barrier, 255)

    def send_all():
        def send(i, _):
            j = lax.rem(i, 8)
            r = i // 8
            half = (j + 1) // 2
            dz = lax.rem(jnp.where(lax.rem(j, 2) == 1, half, 8 - half), 8)
            e = index(lax.rem(z + dz, 8), lax.rem(y + r // 4, 4), lax.rem(x + r, 4), lax.rem(k + r // 16, 2))

            @pl.when(offset(e) <= 60)
            def _():
                remote(amps.at[pl.ds(first_tile(e), TILES - 1)], buf.at[phase_me, pl.ds(0, TILES - 1), slot], send20, recv.at[phase_me], e).start()

            @pl.when(offset(e) > 60)
            def _():
                remote(amps.at[pl.ds(first_tile(e), TILES)], buf.at[phase_me, pl.ds(0, TILES), slot], send21, recv.at[phase_me], e).start()

            return 0

        lax.fori_loop(1, 256, send, 0)

    def sent_all():
        for cond, fewer, more in ((short, 127, 128), (jnp.logical_not(short), 128, 127)):
            @pl.when(cond)
            def _(fewer=fewer, more=more):
                for sem, n in ((send20, fewer * (TILES - 1)), (send21, more * TILES)):
                    part = amps.at[pl.ds(0, n)]
                    remote(part, part, sem, recv.at[0], mate).wait_send()

    @pl.when(phase_me == 0)
    def _():
        send_all()

    load_ints.wait()
    lane = lax.broadcasted_iota(jnp.int32, (32, LANES), 1)
    take = lane >= shift
    tail = lane < WIDTH - 19 * LANES

    for a in range(2):
        def prepare(i, _):
            r = pl.multiple_of(i * 32, 32)
            before = jnp.zeros((32, LANES), jnp.float32)
            for c in range(TILES):
                if c < TILES - 2:
                    v = stage[a, pl.ds(r, 32), c * LANES:(c + 1) * LANES].astype(jnp.float32)
                elif c == TILES - 2:
                    v = stage[a, pl.ds(r, 32), c * LANES:WIDTH].astype(jnp.float32)
                    v = jnp.concatenate([v, jnp.zeros((32, TILES * LANES - LANES - WIDTH), jnp.float32)], axis=1)
                now = pltpu.roll(v, shift, 1) if c < TILES - 1 else jnp.zeros((32, LANES), jnp.float32)
                weights[pl.ds(a * 800 + r, 32), c * LANES:(c + 1) * LANES] = jnp.where(take, now, before).astype(jnp.bfloat16)
                before = now
            return 0

        lax.fori_loop(0, 25, prepare, 0)
    weights[ROWS:, :] = jnp.zeros((WIDE - ROWS, TILES * LANES), jnp.bfloat16)

    def arrived(p):
        for n, cond in ((TILES - 1, short), (TILES, jnp.logical_not(short))):
            def some(count, n=n):
                part = amps.at[pl.ds(0, n * count)]
                remote(part, part, send20, recv.at[p], mate).wait_recv()

            @pl.when(jnp.logical_and(cond, phase_me == p))
            def _(n=n, some=some):
                own_copy(n).wait()
                some(63)

            @pl.when(jnp.logical_and(cond, phase_me != p))
            def _(some=some):
                some(64)

    def multiply(p):
        arrived(p)
        left = jnp.concatenate([buf[p, c].reshape(2 * SOURCES, LANES) for c in range(TILES)], axis=1)
        for n in range(0, WIDE, CHUNK):
            size = min(CHUNK, WIDE - n)
            product[p, :, n:n + size] = lax.dot_general(
                left, weights[n:n + size, :], (((1,), (1,)), ((), ())), preferred_element_type=jnp.float32
            )
            remote(
                product.at[p, pl.ds(pl.multiple_of(64 * (1 - k), 64), 64), pl.ds(n, size)], pair_in.at[p, :, pl.ds(n, size)],
                pair_s, pair_r.at[p], mate,
            ).start()
        remote(pair_in.at[p], pair_in.at[p], pair_s, pair_r.at[p], mate).wait_recv()
        for b in range(8):
            r = pl.multiple_of(64 * k + 8 * b, 8)
            sums[p, b] = product[p, pl.ds(r, 8), :] + pair_in[p, 8 * b:8 * b + 8, :]
            ty, tx = b // 2, 2 * k + b % 2

            @pl.when(jnp.logical_or(ty != y, tx != x))
            def _(b=b, ty=ty, tx=tx):
                remote(sums.at[p, b], plane_in.at[p, y * 4 + x], plane_s, plane_r.at[p], index(z, ty, tx, k)).start()

    def gather(p):
        @pl.when(xh == k)
        def _():
            plane_in[p, y * 4 + x] = sums[p, y * 2 + lax.rem(x, 2)]
            got = plane_in.at[p, pl.ds(0, 15)]
            remote(got, got, plane_s, plane_r.at[p], mate).wait_recv()
            total = plane_in[p, 0]
            for s in range(1, 16):
                total = total + plane_in[p, s]
            kp, q = p // 2, lax.rem(p, 2)
            zl = lax.rem(q + x + y, 2)
            for zh in range(4):
                z_out[4 * p + zh] = total[2 * zh:2 * zh + 2]
                owner = index(2 * zh + zl, y, x, kp)

                @pl.when(owner == me)
                def _(zh=zh):
                    z_in[z] = total[2 * zh:2 * zh + 2]

                @pl.when(owner != me)
                def _(zh=zh, owner=owner):
                    remote(z_out.at[4 * p + zh], z_in.at[z], z_s, z_r, owner).start()

    def step(p, _):
        @pl.when(jnp.logical_and(phase_me == p, p > 0))
        def _():
            pl.semaphore_wait(go, 1)
            send_all()

        @pl.when(jnp.logical_and(p >= 1, p <= PHASES))
        def _():
            multiply(p - 1)

        @pl.when(p >= 2)
        def _():
            gather(p - 2)

        @pl.when(phase_me == p)
        def _():
            sent_all()

            @pl.when(p < PHASES - 1)
            def _():
                follower = index(z, y, x + 1 - 2 * lax.rem(x, 2), (p + 1) // 2)
                pl.semaphore_signal(go, inc=1, device_id=place(follower), device_id_type=MESH)

        return 0

    lax.fori_loop(0, PHASES + 2, step, 0)

    for cond, count in ((xh == k, 7), (xh != k, 8)):
        @pl.when(cond)
        def _(count=count):
            got = z_in.at[pl.ds(0, count)]
            remote(got, got, z_s, z_r, mate).wait_recv()

    total = z_in[0]
    for s in range(1, 8):
        total = total + z_in[s]
    out[:, 0, :] = total[:, 0:800]
    out[:, 1, :] = total[:, 800:1600]

    remote(pair_in, pair_in, pair_s, pair_r.at[0], mate).wait_send()
    for cond, count in ((xh == k, 7), (xh != k, 8)):
        @pl.when(cond)
        def _(count=count):
            part = sums.at[:, pl.ds(0, count)]
            remote(part, part, plane_s, plane_r.at[0], mate).wait_send()

    @pl.when(xh == k)
    def _():
        part = z_out.at[pl.ds(0, 15)]
        remote(part, part, z_s, z_r, mate).wait_send()


def shards(amplitudes, integrals):
    tiles = amplitudes.reshape(2, 5000, LANES).transpose(1, 0, 2)
    dma = pltpu.SemaphoreType.DMA
    return pl.pallas_call(
        kernel,
        out_shape=jax.ShapeDtypeStruct((2, 2, 800), jnp.float32),
        in_specs=[pl.BlockSpec(memory_space=pl.ANY), pl.BlockSpec(memory_space=pl.ANY)],
        out_specs=pl.BlockSpec(memory_space=pltpu.VMEM),
        scratch_shapes=[
            pltpu.VMEM((PHASES, TILES, SOURCES, 2, LANES), jnp.bfloat16),
            pltpu.VMEM((2, 800, WIDTH), jnp.bfloat16),
            pltpu.VMEM((WIDE, TILES * LANES), jnp.bfloat16),
            pltpu.VMEM((PHASES, 128, WIDE), jnp.float32),
            pltpu.VMEM((PHASES, 64, WIDE), jnp.float32),
            pltpu.VMEM((PHASES, 8, 8, WIDE), jnp.float32),
            pltpu.VMEM((PHASES, 16, 8, WIDE), jnp.float32),
            pltpu.VMEM((PHASES * 4, 2, WIDE), jnp.float32),
            pltpu.VMEM((8, 2, WIDE), jnp.float32),
            dma, dma, dma((PHASES,)), pltpu.SemaphoreType.REGULAR, dma, dma,
            dma, dma((PHASES,)), dma, dma((PHASES,)), dma, dma,
        ],
        compiler_params=pltpu.CompilerParams(collective_id=1, has_side_effects=True, vmem_limit_bytes=60 << 20),
        name="ladder",
    )(tiles, integrals)


def solution(mesh):
    return jax.shard_map(
        shards,
        mesh=mesh,
        in_specs=(P(("row", "col"), None), P(None, None, ("row", "col"))),
        out_specs=P(("row", "col"), None, None),
        check_vma=False,
    )
```

```python
import functools

import jax
import jax.numpy as jnp
from jax import lax
from jax.experimental import pallas as pl
from jax.experimental.pallas import tpu as pltpu
from jax.sharding import PartitionSpec as P

FLAT = pl.DeviceIdType.LOGICAL
LANES = 128
WIDTH = 2500
TILES = 21
ROWS = 1600
WIDE = 1664
PHASES = 4
SOURCES = 64
CHUNK = 256
CUTS = ((0, 1024), (1024, WIDE))
GO = ("start", "end", "start")


def index(z, y, x, k):
    return (z >> 1) * 64 + x * 16 + k * 8 + y * 2 + (z & 1)


def kernel(
    amps, ints, out, buf, stage, weights, product, pair_in, sums, plane_in, z_out, z_in,
    send_s, recv, go, own, load, pair_s, pair_r, plane_s, plane_r, z_s, z_r,
):
    row, col = lax.axis_index("row"), lax.axis_index("col")
    me = row * 8 + col
    z = (row >> 3) * 2 + (col & 1)
    x = (row >> 1) & 3
    k = row & 1
    y = col >> 1
    parity = (x + y + z) & 1
    phase_me = 2 * k + parity
    xh = x >> 1
    slot = ((xh * 4 + y) * 2 + (x & 1)) * 4 + (z >> 1)
    mate = index(z, y, x, 1 - k)

    def first_tile(e):
        return (e * WIDTH) >> 7

    def offset(e):
        return (e * WIDTH) & (LANES - 1)

    def remote(src, dst, ssem, rsem, device):
        return pltpu.make_async_remote_copy(src, dst, ssem, rsem, device_id=device, device_id_type=FLAT)

    barrier = pltpu.get_barrier_semaphore()

    def greet(i, _):
        gz, gy = i >> 3, (i >> 1) & 3
        e = index(gz, gy, (i & 1) * 2 + ((gy + gz) & 1), 0)

        @pl.when(e != me)
        def _():
            pl.semaphore_signal(barrier, inc=1, device_id=e, device_id_type=FLAT)

        return 0

    lax.fori_loop(0, SOURCES, greet, 0)
    shift = offset(me)
    short = shift <= 60
    load_ints = pltpu.make_async_copy(ints, stage, load)
    load_ints.start()

    @pl.when(short)
    def _():
        for p in range(PHASES):
            buf[p, TILES - 1] = jnp.zeros((SOURCES, 2, LANES), jnp.bfloat16)

    def own_copy(n):
        return pltpu.make_async_copy(amps.at[pl.ds(first_tile(me), n)], buf.at[phase_me, pl.ds(0, n), slot], own)

    @pl.when(short)
    def _():
        own_copy(TILES - 1).start()

    @pl.when(jnp.logical_not(short))
    def _():
        own_copy(TILES).start()

    @pl.when(phase_me == 0)
    def _():
        pl.semaphore_wait(barrier, 255)

    def send(e, half):
        def some(n, kind):
            remote(
                amps.at[pl.ds(first_tile(e), n)], buf.at[phase_me, pl.ds(0, n), slot], send_s.at[half, kind], recv.at[phase_me], e
            ).start()

        lax.cond(offset(e) <= 60, lambda: some(TILES - 1, 0), lambda: some(TILES, 1))

    def send_all():
        layers = [index((z + dz) & 7, 0, 0, 0) for dz in (1, 7, 2, 6, 3, 5, 4, 0)]
        for layer in layers[:7]:
            send(layer + index(0, y, x, k), 0)
        for half in range(2):
            def plane(r, _, half=half):
                base = index(0, (y + (r >> 2)) & 3, (x + r) & 3, (k + half) & 1)
                for layer in layers:
                    send(layer + base, half)
                return 0

            lax.fori_loop(1 - half, 16, plane, 0)

    def sent(half):
        for cond, fewer, more in ((short, 63, 64), (jnp.logical_not(short), 64, 63)):
            @pl.when(cond)
            def _(fewer=fewer, more=more):
                for kind, n in ((0, (64 if half else fewer) * (TILES - 1)), (1, (64 if half else more) * TILES)):
                    part = amps.at[pl.ds(0, n)]
                    remote(part, part, send_s.at[half, kind], recv.at[0], mate).wait_send()

    def pass_on(p):
        follower = index(z, y, x + 1 - 2 * (x & 1), (p + 1) >> 1)
        pl.semaphore_signal(go, inc=1, device_id=follower, device_id_type=FLAT)

    @pl.when(phase_me == 0)
    def _():
        if GO[0] == "start":
            pass_on(0)
        send_all()

    load_ints.wait()

    def prepare(r, count):
        lane = lax.broadcasted_iota(jnp.int32, (count, LANES), 1)
        take = lane >= shift
        before = jnp.zeros((count, LANES), jnp.float32)
        for c in range(TILES):
            if c < TILES - 2:
                v = stage[pl.ds(r, count), c * LANES:(c + 1) * LANES].astype(jnp.float32)
            elif c == TILES - 2:
                v = stage[pl.ds(r, count), c * LANES:WIDTH].astype(jnp.float32)
                v = jnp.concatenate([v, jnp.zeros((count, TILES * LANES - LANES - WIDTH), jnp.float32)], axis=1)
            now = pltpu.roll(v, shift, 1) if c < TILES - 1 else jnp.zeros((count, LANES), jnp.float32)
            block = jnp.where(take, now, before)
            if count < LANES:
                block = jnp.concatenate([block, jnp.zeros((LANES - count, LANES), jnp.float32)], axis=0)
            weights[c * LANES:(c + 1) * LANES, pl.ds(r, LANES)] = block.T.astype(jnp.bfloat16)
            before = now

    def prepare_block(i, _):
        prepare(pl.multiple_of(i * LANES, LANES), LANES)
        return 0

    lax.fori_loop(0, ROWS // LANES, prepare_block, 0)
    prepare(ROWS // LANES * LANES, ROWS % LANES)

    def arrived(p):
        for n, cond in ((TILES - 1, short), (TILES, jnp.logical_not(short))):
            def some(count, n=n):
                part = amps.at[pl.ds(0, n * count)]
                remote(part, part, send_s.at[0, 0], recv.at[p], mate).wait_recv()

            @pl.when(jnp.logical_and(cond, phase_me == p))
            def _(n=n, some=some):
                own_copy(n).wait()
                some(63)

            @pl.when(jnp.logical_and(cond, phase_me != p))
            def _(some=some):
                some(64)

    def multiply(p):
        arrived(p)
        left = jnp.concatenate([buf[p, c].reshape(2 * SOURCES, LANES) for c in range(TILES)], axis=1)
        theirs = pl.multiple_of(64 * (1 - k), 64)
        for cut, (lo, hi) in enumerate(CUTS):
            for n in range(lo, hi, CHUNK):
                size = min(CHUNK, hi - n)
                product[p, :, n:n + size] = jnp.dot(left, weights[:, n:n + size], preferred_element_type=jnp.float32)
            remote(
                product.at[p, pl.ds(theirs, 64), pl.ds(lo, hi - lo)], pair_in.at[p, :, pl.ds(lo, hi - lo)],
                pair_s, pair_r.at[p, cut], mate,
            ).start()
        for cut, (lo, hi) in enumerate(CUTS):
            got = pair_in.at[p, :, pl.ds(lo, hi - lo)]
            remote(got, got, pair_s, pair_r.at[p, cut], mate).wait_recv()
            for b in range(8):
                r = pl.multiple_of(64 * k + 8 * b, 8)
                sums[p, b, :, lo:hi] = product[p, pl.ds(r, 8), lo:hi] + pair_in[p, 8 * b:8 * b + 8, lo:hi]
                ty, tx = b // 2, 2 * k + b % 2

                @pl.when(jnp.logical_or(ty != y, tx != x))
                def _(b=b, ty=ty, tx=tx):
                    remote(
                        sums.at[p, b, :, pl.ds(lo, hi - lo)], plane_in.at[p, y * 4 + x, :, pl.ds(lo, hi - lo)],
                        plane_s, plane_r.at[p, cut], index(z, ty, tx, k),
                    ).start()

    def gather(p):
        @pl.when(xh == k)
        def _():
            plane_in[p, y * 4 + x] = sums[p, y * 2 + (x & 1)]
            for cut, (lo, hi) in enumerate(CUTS):
                got = plane_in.at[p, pl.ds(0, 15), :, pl.ds(lo, hi - lo)]
                remote(got, got, plane_s, plane_r.at[p, cut], mate).wait_recv()
            total = plane_in[p, 0]
            for s in range(1, 16):
                total = total + plane_in[p, s]
            kp, q = p >> 1, p & 1
            zl = (q + x + y) & 1
            for zh in range(4):
                z_out[4 * p + zh] = total[2 * zh:2 * zh + 2]
                owner = index(2 * zh + zl, y, x, kp)

                @pl.when(owner == me)
                def _(zh=zh):
                    z_in[z] = total[2 * zh:2 * zh + 2]

                @pl.when(owner != me)
                def _(zh=zh, owner=owner):
                    remote(z_out.at[4 * p + zh], z_in.at[z], z_s, z_r, owner).start()

    def step(p, _):
        @pl.when(jnp.logical_and(phase_me == p, p > 0))
        def _():
            pl.semaphore_wait(go, 1)
            for q in range(1, PHASES - 1):
                if GO[q] == "start":
                    @pl.when(p == q)
                    def _(q=q):
                        pass_on(q)
            send_all()

        @pl.when(jnp.logical_and(p >= 1, p <= PHASES))
        def _():
            multiply(p - 1)

        @pl.when(phase_me == p)
        def _():
            sent(0)
            for q in range(PHASES - 1):
                if GO[q] == "half":
                    @pl.when(p == q)
                    def _(q=q):
                        pass_on(q)
            sent(1)
            for q in range(PHASES - 1):
                if GO[q] == "end":
                    @pl.when(p == q)
                    def _(q=q):
                        pass_on(q)

        @pl.when(p >= 2)
        def _():
            gather(p - 2)

        return 0

    lax.fori_loop(0, PHASES + 2, step, 0)

    for cond, count in ((xh == k, 7), (xh != k, 8)):
        @pl.when(cond)
        def _(count=count):
            got = z_in.at[pl.ds(0, count)]
            remote(got, got, z_s, z_r, mate).wait_recv()

    total = z_in[0]
    for s in range(1, 8):
        total = total + z_in[s]
    out[:, 0, :] = total[:, 0:800]
    out[:, 1, :] = total[:, 800:1600]

    remote(pair_in, pair_in, pair_s, pair_r.at[0, 0], mate).wait_send()
    for cond, count in ((xh == k, 7), (xh != k, 8)):
        @pl.when(cond)
        def _(count=count):
            part = sums.at[:, pl.ds(0, count)]
            remote(part, part, plane_s, plane_r.at[0, 0], mate).wait_send()

    @pl.when(xh == k)
    def _():
        part = z_out.at[pl.ds(0, 15)]
        remote(part, part, z_s, z_r, mate).wait_send()


def shards(amplitudes, integrals):
    tiles = amplitudes.reshape(2, 5000, LANES).transpose(1, 0, 2)
    dma = pltpu.SemaphoreType.DMA
    return pl.pallas_call(
        kernel,
        out_shape=jax.ShapeDtypeStruct((2, 2, 800), jnp.float32),
        in_specs=[pl.BlockSpec(memory_space=pl.ANY), pl.BlockSpec(memory_space=pl.ANY)],
        out_specs=pl.BlockSpec(memory_space=pltpu.VMEM),
        scratch_shapes=[
            pltpu.VMEM((PHASES, TILES, SOURCES, 2, LANES), jnp.bfloat16),
            pltpu.VMEM((ROWS, WIDTH), jnp.bfloat16),
            pltpu.VMEM((TILES * LANES, WIDE), jnp.bfloat16),
            pltpu.VMEM((PHASES, 128, WIDE), jnp.float32),
            pltpu.VMEM((PHASES, 64, WIDE), jnp.float32),
            pltpu.VMEM((PHASES, 8, 8, WIDE), jnp.float32),
            pltpu.VMEM((PHASES, 16, 8, WIDE), jnp.float32),
            pltpu.VMEM((PHASES * 4, 2, WIDE), jnp.float32),
            pltpu.VMEM((8, 2, WIDE), jnp.float32),
            dma((2, 2)), dma((PHASES,)), pltpu.SemaphoreType.REGULAR, dma, dma,
            dma, dma((PHASES, 2)), dma, dma((PHASES, 2)), dma, dma,
        ],
        compiler_params=pltpu.CompilerParams(collective_id=1, has_side_effects=True, vmem_limit_bytes=60 << 20),
        name="ladder",
    )(tiles, integrals.reshape(ROWS, WIDTH))


def solution(mesh):
    return jax.shard_map(
        shards,
        mesh=mesh,
        in_specs=(P(("row", "col"), None), P(None, None, ("row", "col"))),
        out_specs=P(("row", "col"), None, None),
        check_vma=False,
    )
```

```python
import functools

import jax
import jax.numpy as jnp
from jax import lax
from jax.experimental import pallas as pl
from jax.experimental.pallas import tpu as pltpu
from jax.sharding import PartitionSpec as P

FLAT = pl.DeviceIdType.LOGICAL
LANES = 128
WIDTH = 2500
TILES = 21
ROWS = 1600
WIDE = 1664
PHASES = 4
SOURCES = 64
CHUNK = 256
CUTS = ((0, 768), (768, WIDE))
FIRST = 28
WAITS = (0, 0)


def index(z, y, x, k):
    return (z >> 1) * 64 + x * 16 + k * 8 + y * 2 + (z & 1)


def kernel(
    amps, ints, out, buf, stage, weights, product, pair_in, x_out, x_in, xy_out, xy_in, y_out, y_in, yx_out, yx_in, z_out, z_in,
    send_s, recv, go, own, load, pair_s, pair_r, x_s, x_r, xy_s, xy_r, y_s, y_r, yx_s, yx_r, z_s, z_r,
):
    row, col = lax.axis_index("row"), lax.axis_index("col")
    me = row * 8 + col
    z = (row >> 3) * 2 + (col & 1)
    x = (row >> 1) & 3
    k = row & 1
    y = col >> 1
    parity = (x + y + z) & 1
    phase_me = 2 * k + parity
    xh = x >> 1
    slot = ((xh * 4 + y) * 2 + (x & 1)) * 4 + (z >> 1)
    mate = index(z, y, x, 1 - k)

    def first_tile(e):
        return (e * WIDTH) >> 7

    def offset(e):
        return (e * WIDTH) & (LANES - 1)

    def remote(src, dst, ssem, rsem, device):
        return pltpu.make_async_remote_copy(src, dst, ssem, rsem, device_id=device, device_id_type=FLAT)

    barrier = pltpu.get_barrier_semaphore()

    def greet(i, _):
        gz, gy = i >> 3, (i >> 1) & 3
        e = index(gz, gy, (i & 1) * 2 + ((gy + gz) & 1), 0)

        @pl.when(e != me)
        def _():
            pl.semaphore_signal(barrier, inc=1, device_id=e, device_id_type=FLAT)

        return 0

    lax.fori_loop(0, SOURCES, greet, 0)
    shift = offset(me)
    short = shift <= 60
    load_ints = pltpu.make_async_copy(ints, stage, load)
    load_ints.start()

    @pl.when(short)
    def _():
        for p in range(PHASES):
            buf[p, TILES - 1] = jnp.zeros((SOURCES, 2, LANES), jnp.bfloat16)

    def own_copy(n):
        return pltpu.make_async_copy(amps.at[pl.ds(first_tile(me), n)], buf.at[phase_me, pl.ds(0, n), slot], own)

    @pl.when(short)
    def _():
        own_copy(TILES - 1).start()

    @pl.when(jnp.logical_not(short))
    def _():
        own_copy(TILES).start()

    @pl.when(phase_me == 0)
    def _():
        pl.semaphore_wait(barrier, 255)

    def send(e, half):
        def some(n, kind):
            remote(
                amps.at[pl.ds(first_tile(e), n)], buf.at[phase_me, pl.ds(0, n), slot], send_s.at[half, kind], recv.at[phase_me], e
            ).start()

        lax.cond(offset(e) <= 60, lambda: some(TILES - 1, 0), lambda: some(TILES, 1))

    def send_all():
        near = [[index((z + dz) & 7, 0, 0, 0) for dz in pair] for pair in ((1, 7), (2, 6), (3, 5), (4, 0))]
        turns = (5, 10, 15, 0)

        def group(i, part, first=False):
            for pair, turn in zip(near, turns):
                r = i + turn
                base = index(0, (y + r + ((r & 15) >> 2)) & 3, (x + r) & 3, (k + (i >> 4)) & 1)
                for layer in pair[:1] if first and turn == 0 else pair:
                    send(layer + base, part)

        group(0, 0, True)
        for part, (lo, hi) in enumerate(((1, FIRST), (FIRST, 32))):
            def turn(i, _, part=part):
                group(i, part)
                return 0

            lax.fori_loop(lo, hi, turn, 0)

    def sent(part):
        count = (4 * FIRST, 128 - 4 * FIRST)[part]
        for cond, fewer in ((short, 0), (jnp.logical_not(short), 1)):
            @pl.when(cond)
            def _(fewer=fewer):
                for kind, n in ((0, TILES - 1), (1, TILES)):
                    less = 1 if part == 0 and kind == fewer else 0
                    moved = amps.at[pl.ds(0, n * (count - less))]
                    remote(moved, moved, send_s.at[part, kind], recv.at[0], mate).wait_send()

    def signal(device):
        pl.semaphore_signal(go, inc=1, device_id=device, device_id_type=FLAT)

    @pl.when(phase_me == 0)
    def _():
        signal(index(z, y, x + 1 - 2 * (x & 1), 0))

    @pl.when(phase_me == 1)
    def _():
        pl.semaphore_wait(go, 1)

    @pl.when(k == 0)
    def _():
        send_all()

    load_ints.wait()

    def prepare(r, count):
        lane = lax.broadcasted_iota(jnp.int32, (count, LANES), 1)
        take = lane >= shift
        before = jnp.zeros((count, LANES), jnp.float32)
        for c in range(TILES):
            if c < TILES - 2:
                v = stage[pl.ds(r, count), c * LANES:(c + 1) * LANES].astype(jnp.float32)
            elif c == TILES - 2:
                v = stage[pl.ds(r, count), c * LANES:WIDTH].astype(jnp.float32)
                v = jnp.concatenate([v, jnp.zeros((count, TILES * LANES - LANES - WIDTH), jnp.float32)], axis=1)
            now = pltpu.roll(v, shift, 1) if c < TILES - 1 else jnp.zeros((count, LANES), jnp.float32)
            block = jnp.where(take, now, before)
            if count < LANES:
                block = jnp.concatenate([block, jnp.zeros((LANES - count, LANES), jnp.float32)], axis=0)
            weights[c * LANES:(c + 1) * LANES, pl.ds(r, LANES)] = block.T.astype(jnp.bfloat16)
            before = now

    def prepare_block(i, _):
        prepare(pl.multiple_of(i * LANES, LANES), LANES)
        return 0

    lax.fori_loop(0, ROWS // LANES, prepare_block, 0)
    prepare(ROWS // LANES * LANES, ROWS % LANES)

    def arrived(p):
        for n, cond in ((TILES - 1, short), (TILES, jnp.logical_not(short))):
            def some(count, n=n):
                part = amps.at[pl.ds(0, n * count)]
                remote(part, part, send_s.at[0, 0], recv.at[p], mate).wait_recv()

            @pl.when(jnp.logical_and(cond, phase_me == p))
            def _(n=n, some=some):
                own_copy(n).wait()
                some(63)

            @pl.when(jnp.logical_and(cond, phase_me != p))
            def _(some=some):
                some(64)

    def multiply(p):
        arrived(p)
        left = jnp.concatenate([buf[p, c].reshape(2 * SOURCES, LANES) for c in range(TILES)], axis=1)
        theirs = pl.multiple_of(64 * (1 - k), 64)
        for cut, (lo, hi) in enumerate(CUTS):
            for n in range(lo, hi, CHUNK):
                size = min(CHUNK, hi - n)
                product[p, :, n:n + size] = jnp.dot(left, weights[:, n:n + size], preferred_element_type=jnp.float32)
            remote(
                product.at[p, pl.ds(theirs, 64), pl.ds(lo, hi - lo)], pair_in.at[p, :, pl.ds(lo, hi - lo)],
                pair_s, pair_r.at[p, cut], mate,
            ).start()

    def combine(p):
        for cut, (lo, hi) in enumerate(CUTS):
            got = pair_in.at[p, :, pl.ds(lo, hi - lo)]
            remote(got, got, pair_s, pair_r.at[p, cut], mate).wait_recv()
            for ty in range(4):
                for xl in range(2):
                    r = 16 * ty + 8 * xl
                    total = product[p, pl.ds(pl.multiple_of(64 * k + r, 8), 8), lo:hi] + pair_in[p, r:r + 8, lo:hi]
                    if cut == 0:
                        x_out[p, xl, ty] = total
                    else:
                        y_out[p, ty, xl] = total
            if cut == 0:
                for xl in range(2):
                    @pl.when(2 * k + xl != x)
                    def _(xl=xl):
                        remote(x_out.at[p, xl], x_in.at[p, x], x_s, x_r.at[p], index(z, y, 2 * k + xl, k)).start()
            else:
                for ty in range(4):
                    @pl.when(ty != y)
                    def _(ty=ty):
                        remote(y_out.at[p, ty], y_in.at[p, y], y_s, y_r.at[p], index(z, ty, x, k)).start()

    def received(n, sem):
        part = amps.at[pl.ds(0, n)]
        remote(part, part, pair_s, sem, mate).wait_recv()

    def departed(n, sem):
        part = amps.at[pl.ds(0, n)]
        remote(part, part, sem, pair_r.at[0, 0], mate).wait_send()

    X, Y = CUTS[0][1], WIDE - CUTS[0][1]

    def middle(p):
        @pl.when(xh == k)
        def _():
            x_in[p, x] = x_out[p, x & 1]
            received(3 * X // 4, x_r.at[p])
            for ty in range(4):
                total = (x_in[p, 0, ty] + x_in[p, 1, ty]) + (x_in[p, 2, ty] + x_in[p, 3, ty])
                xy_out[p, ty] = total

                @pl.when(ty != y)
                def _(ty=ty):
                    remote(xy_out.at[p, ty], xy_in.at[p, y], xy_s, xy_r.at[p], index(z, ty, x, k)).start()

        y_in[p, y] = y_out[p, y]
        received(3 * Y // 8, y_r.at[p])
        for xl in range(2):
            total = (y_in[p, 0, xl] + y_in[p, 1, xl]) + (y_in[p, 2, xl] + y_in[p, 3, xl])
            yx_out[p, xl] = total

            @pl.when(2 * k + xl != x)
            def _(xl=xl):
                remote(yx_out.at[p, xl], yx_in.at[p, x], yx_s, yx_r.at[p], index(z, y, 2 * k + xl, k)).start()

    def gather(p):
        @pl.when(xh == k)
        def _():
            xy_in[p, y] = xy_out[p, y]
            yx_in[p, x] = yx_out[p, x & 1]
            received(3 * X // 16, xy_r.at[p])
            received(3 * Y // 16, yx_r.at[p])
            first = (xy_in[p, 0] + xy_in[p, 1]) + (xy_in[p, 2] + xy_in[p, 3])
            second = (yx_in[p, 0] + yx_in[p, 1]) + (yx_in[p, 2] + yx_in[p, 3])
            total = jnp.concatenate([first, second], axis=1)
            kp, q = p >> 1, p & 1
            zl = (q + x + y) & 1
            for zh in range(4):
                z_out[4 * p + zh] = total[2 * zh:2 * zh + 2]
                owner = index(2 * zh + zl, y, x, kp)

                @pl.when(owner == me)
                def _(zh=zh):
                    z_in[z] = total[2 * zh:2 * zh + 2]

                @pl.when(owner != me)
                def _(zh=zh, owner=owner):
                    remote(z_out.at[4 * p + zh], z_in.at[z], z_s, z_r, owner).start()

    @pl.when(k == 0)
    def _():
        sent(0)
        for q in range(2):
            @pl.when(parity == q)
            def _(q=q):
                if WAITS[q] == 0:
                    signal(mate)
                    sent(1)
                else:
                    sent(1)
                    signal(mate)

    @pl.when(k == 1)
    def _():
        pl.semaphore_wait(go, 1)
        send_all()

    def each(f, lo):
        def one(p, _):
            f(p)
            return 0

        lax.fori_loop(lo, lo + 2, one, 0)

    each(multiply, 0)
    each(combine, 0)
    each(middle, 0)

    def both(p):
        multiply(p)
        combine(p)

    @pl.when(k == 0)
    def _():
        each(both, 2)

    @pl.when(k == 1)
    def _():
        each(multiply, 2)
        each(combine, 2)

    each(gather, 0)
    each(middle, 2)
    each(gather, 2)

    for cond, count in ((xh == k, 7), (xh != k, 8)):
        @pl.when(cond)
        def _(count=count):
            got = z_in.at[pl.ds(0, count)]
            remote(got, got, z_s, z_r, mate).wait_recv()

    total = z_in[0]
    for s in range(1, 8):
        total = total + z_in[s]
    out[:, 0, :] = total[:, 0:800]
    out[:, 1, :] = total[:, 800:1600]

    @pl.when(k == 1)
    def _():
        sent(0)
        sent(1)

    remote(pair_in, pair_in, pair_s, pair_r.at[0, 0], mate).wait_send()
    departed(4 * 3 * Y // 8, y_s)
    for cond, count in ((xh == k, 1), (xh != k, 2)):
        @pl.when(cond)
        def _(count=count):
            departed(4 * count * X // 4, x_s)
            departed(4 * count * Y // 16, yx_s)

    @pl.when(xh == k)
    def _():
        departed(4 * 3 * X // 16, xy_s)

    @pl.when(xh == k)
    def _():
        part = z_out.at[pl.ds(0, 15)]
        remote(part, part, z_s, z_r, mate).wait_send()


def shards(amplitudes, integrals):
    tiles = amplitudes.reshape(2, 5000, LANES).transpose(1, 0, 2)
    dma = pltpu.SemaphoreType.DMA
    return pl.pallas_call(
        kernel,
        out_shape=jax.ShapeDtypeStruct((2, 2, 800), jnp.float32),
        in_specs=[pl.BlockSpec(memory_space=pl.ANY), pl.BlockSpec(memory_space=pl.ANY)],
        out_specs=pl.BlockSpec(memory_space=pltpu.VMEM),
        scratch_shapes=[
            pltpu.VMEM((PHASES, TILES, SOURCES, 2, LANES), jnp.bfloat16),
            pltpu.VMEM((ROWS, WIDTH), jnp.bfloat16),
            pltpu.VMEM((TILES * LANES, WIDE), jnp.bfloat16),
            pltpu.VMEM((PHASES, 128, WIDE), jnp.float32),
            pltpu.VMEM((PHASES, 64, WIDE), jnp.float32),
            pltpu.VMEM((PHASES, 2, 4, 8, CUTS[0][1]), jnp.float32),
            pltpu.VMEM((PHASES, 4, 4, 8, CUTS[0][1]), jnp.float32),
            pltpu.VMEM((PHASES, 4, 8, CUTS[0][1]), jnp.float32),
            pltpu.VMEM((PHASES, 4, 8, CUTS[0][1]), jnp.float32),
            pltpu.VMEM((PHASES, 4, 2, 8, WIDE - CUTS[0][1]), jnp.float32),
            pltpu.VMEM((PHASES, 4, 2, 8, WIDE - CUTS[0][1]), jnp.float32),
            pltpu.VMEM((PHASES, 2, 8, WIDE - CUTS[0][1]), jnp.float32),
            pltpu.VMEM((PHASES, 4, 8, WIDE - CUTS[0][1]), jnp.float32),
            pltpu.VMEM((PHASES * 4, 2, WIDE), jnp.float32),
            pltpu.VMEM((8, 2, WIDE), jnp.float32),
            dma((2, 2)), dma((PHASES,)), pltpu.SemaphoreType.REGULAR, dma, dma,
            dma, dma((PHASES, 2)), dma, dma((PHASES,)), dma, dma((PHASES,)), dma, dma((PHASES,)), dma, dma((PHASES,)), dma, dma,
        ],
        compiler_params=pltpu.CompilerParams(collective_id=1, has_side_effects=True, vmem_limit_bytes=60 << 20),
        name="ladder",
    )(tiles, integrals.reshape(ROWS, WIDTH))


def solution(mesh):
    return jax.shard_map(
        shards,
        mesh=mesh,
        in_specs=(P(("row", "col"), None), P(None, None, ("row", "col"))),
        out_specs=P(("row", "col"), None, None),
        check_vma=False,
    )
```

```python
import functools

import jax
import jax.numpy as jnp
from jax import lax
from jax.experimental import pallas as pl
from jax.experimental.pallas import tpu as pltpu
from jax.sharding import PartitionSpec as P

FLAT = pl.DeviceIdType.LOGICAL
LANES = 128
WIDTH = 2500
TILES = 20
ROWS = 1600
WIDE = 1664
PHASES = 4
SOURCES = 64
CHUNK = 256
CUTS = ((0, 768), (768, WIDE))


def index(z, y, x, k):
    return (z >> 1) * 64 + x * 16 + k * 8 + y * 2 + (z & 1)


def kernel(
    amps, ints, out, buf, merged, stage, weights, product, pair_in, x_out, x_in, xy_out, xy_in, y_out, y_in, yx_out, yx_in, z_out, z_in,
    send_s, recv, go, own, load, load_tiles, pair_s, pair_r, x_s, x_r, xy_s, xy_r, y_s, y_r, yx_s, yx_r, z_s, z_r,
):
    row, col = lax.axis_index("row"), lax.axis_index("col")
    me = row * 8 + col
    z = (row >> 3) * 2 + (col & 1)
    x = (row >> 1) & 3
    k = row & 1
    y = col >> 1
    parity = (x + y + z) & 1
    phase_me = 2 * k + parity
    xh = x >> 1
    slot = ((xh * 4 + y) * 2 + (x & 1)) * 4 + (z >> 1)
    mate = index(z, y, x, 1 - k)

    def first_tile(e):
        return (e * WIDTH) >> 7

    def offset(e):
        return (e * WIDTH) & (LANES - 1)

    def remote(src, dst, ssem, rsem, device):
        return pltpu.make_async_remote_copy(src, dst, ssem, rsem, device_id=device, device_id_type=FLAT)

    barrier = pltpu.get_barrier_semaphore()

    def greet(i, _):
        gz, gy = i >> 3, (i >> 1) & 3
        e = index(gz, gy, (i & 1) * 2 + ((gy + gz) & 1), 0)

        @pl.when(e != me)
        def _():
            pl.semaphore_signal(barrier, inc=1, device_id=e, device_id_type=FLAT)

        return 0

    lax.fori_loop(0, SOURCES, greet, 0)
    shift = offset(me)
    load_ints = pltpu.make_async_copy(ints, stage, load)
    odd = (x + z) & 1

    def fetch(j, _):
        e = 2 * j + 1 - ((j >> 3) & 1)
        pltpu.make_async_copy(amps.at[pl.ds(first_tile(e), TILES + 1)], merged.at[j >> 4, j & 15], load_tiles).start()
        return 0

    def merge():
        part = amps.at[pl.ds(0, 128 * (TILES + 1))]
        pltpu.make_async_copy(part, part, load_tiles).wait()
        lane = lax.broadcasted_iota(jnp.int32, (8, 2, LANES), 2)
        for j in range(16):
            first = lane >= ((2 * j + 1 - (j >> 3)) * WIDTH) % LANES
            head, last = merged[:, j, 0].astype(jnp.float32), merged[:, j, TILES].astype(jnp.float32)
            merged[:, j, 0] = jnp.where(first, head, last).astype(jnp.bfloat16)

    def straight(e):
        return amps.at[pl.ds(first_tile(e), TILES)]

    def folded(e):
        return merged.at[e >> 5, (e >> 1) & 15, pl.ds(0, TILES)]

    def own_copy(src):
        return pltpu.make_async_copy(src, buf.at[phase_me, :, slot], own)

    def send_some(lo, hi, core, fold, part):
        near = [[index((z + dz) & 7, 0, 0, 0) for dz in pair] for pair in ((1, 7), (2, 6), (3, 5), (4, 0))]

        def group(m, last):
            i = 2 * m + (odd ^ fold)
            for pair, turn in zip(near, (5, 10, 15, 0)):
                r = i + turn
                base = index(0, (y + r + ((r & 15) >> 2)) & 3, (x + r) & 3, (k + core) & 1)
                for number, layer in enumerate(pair):
                    e = layer + base

                    def go_to(e=e):
                        src = folded(e) if fold else straight(e)
                        remote(src, buf.at[phase_me, :, slot], send_s.at[part], recv.at[phase_me], e).start()

                    if last and turn == 0 and number == 1:
                        pl.when(e != me)(go_to)
                    else:
                        go_to()

        if lo == 0:
            group(0, core == 0)

        def one(m, _):
            group(m, False)
            return 0

        lax.fori_loop(max(lo, 1), hi, one, 0)

    def send_all():
        send_some(0, 8, 0, 0, 0)
        merge()

        @pl.when(odd == 1)
        def _():
            own_copy(folded(me)).start()

        @pl.when(odd == 0)
        def _():
            own_copy(straight(me)).start()

        send_some(0, 8, 0, 1, 0)
        send_some(0, 8, 1, 0, 0)
        send_some(0, 4, 1, 1, 0)
        send_some(4, 8, 1, 1, 1)

    def sent(part):
        gone = amps.at[pl.ds(0, (223, 32)[part] * TILES)]
        remote(gone, gone, send_s.at[part], recv.at[0], mate).wait_send()

    load_ints.start()
    lax.fori_loop(0, 128, fetch, 0)

    @pl.when(phase_me == 0)
    def _():
        pl.semaphore_wait(barrier, 255)

    def signal(device):
        pl.semaphore_signal(go, inc=1, device_id=device, device_id_type=FLAT)

    @pl.when(phase_me == 0)
    def _():
        signal(index(z, y, x + 1 - 2 * (x & 1), 0))

    @pl.when(phase_me == 1)
    def _():
        pl.semaphore_wait(go, 1)

    @pl.when(k == 0)
    def _():
        send_all()

    load_ints.wait()

    def prepare(r, count):
        take = lax.broadcasted_iota(jnp.int32, (count, LANES), 1) >= shift

        def turned(c):
            v = stage[pl.ds(r, count), c * LANES:min((c + 1) * LANES, WIDTH)].astype(jnp.float32)
            if c == TILES - 1:
                v = jnp.concatenate([v, jnp.zeros((count, TILES * LANES - WIDTH), jnp.float32)], axis=1)
            return pltpu.roll(v, shift, 1)

        before = turned(TILES - 1)
        for c in range(TILES):
            now = turned(c)
            block = jnp.where(take, now, before)
            if count < LANES:
                block = jnp.concatenate([block, jnp.zeros((LANES - count, LANES), jnp.float32)], axis=0)
            weights[c * LANES:(c + 1) * LANES, pl.ds(r, LANES)] = block.T.astype(jnp.bfloat16)
            before = now

    def prepare_block(i, _):
        prepare(pl.multiple_of(i * LANES, LANES), LANES)
        return 0

    lax.fori_loop(0, ROWS // LANES, prepare_block, 0)
    prepare(ROWS // LANES * LANES, ROWS % LANES)

    def arrived(p):
        for cond, count in ((phase_me == p, 63), (phase_me != p, 64)):
            @pl.when(cond)
            def _(count=count):
                part = amps.at[pl.ds(0, TILES * count)]
                remote(part, part, send_s.at[0], recv.at[p], mate).wait_recv()
                if count == 63:
                    own_copy(straight(me)).wait()

    def multiply(p):
        arrived(p)
        left = jnp.concatenate([buf[p, c].reshape(2 * SOURCES, LANES) for c in range(TILES)], axis=1)
        theirs = pl.multiple_of(64 * (1 - k), 64)
        for cut, (lo, hi) in enumerate(CUTS):
            for n in range(lo, hi, CHUNK):
                size = min(CHUNK, hi - n)
                product[p, :, n:n + size] = jnp.dot(left, weights[:, n:n + size], preferred_element_type=jnp.float32)
            remote(
                product.at[p, pl.ds(theirs, 64), pl.ds(lo, hi - lo)], pair_in.at[p, :, pl.ds(lo, hi - lo)],
                pair_s, pair_r.at[p, cut], mate,
            ).start()

    def combine(p):
        for cut, (lo, hi) in enumerate(CUTS):
            got = pair_in.at[p, :, pl.ds(lo, hi - lo)]
            remote(got, got, pair_s, pair_r.at[p, cut], mate).wait_recv()
            for ty in range(4):
                for xl in range(2):
                    r = 16 * ty + 8 * xl
                    total = product[p, pl.ds(pl.multiple_of(64 * k + r, 8), 8), lo:hi] + pair_in[p, r:r + 8, lo:hi]
                    if cut == 0:
                        x_out[p, xl, ty] = total
                    else:
                        y_out[p, ty, xl] = total
            if cut == 0:
                for xl in range(2):
                    @pl.when(2 * k + xl != x)
                    def _(xl=xl):
                        remote(x_out.at[p, xl], x_in.at[p, x], x_s, x_r.at[p], index(z, y, 2 * k + xl, k)).start()
            else:
                for ty in range(4):
                    @pl.when(ty != y)
                    def _(ty=ty):
                        remote(y_out.at[p, ty], y_in.at[p, y], y_s, y_r.at[p], index(z, ty, x, k)).start()

    def received(n, sem):
        part = amps.at[pl.ds(0, n)]
        remote(part, part, pair_s, sem, mate).wait_recv()

    def departed(n, sem):
        part = amps.at[pl.ds(0, n)]
        remote(part, part, sem, pair_r.at[0, 0], mate).wait_send()

    X, Y = CUTS[0][1], WIDE - CUTS[0][1]

    def middle(p):
        @pl.when(xh == k)
        def _():
            x_in[p, x] = x_out[p, x & 1]
            received(3 * X // 4, x_r.at[p])
            for ty in range(4):
                total = (x_in[p, 0, ty] + x_in[p, 1, ty]) + (x_in[p, 2, ty] + x_in[p, 3, ty])
                xy_out[p, ty] = total

                @pl.when(ty != y)
                def _(ty=ty):
                    remote(xy_out.at[p, ty], xy_in.at[p, y], xy_s, xy_r.at[p], index(z, ty, x, k)).start()

        y_in[p, y] = y_out[p, y]
        received(3 * Y // 8, y_r.at[p])
        for xl in range(2):
            total = (y_in[p, 0, xl] + y_in[p, 1, xl]) + (y_in[p, 2, xl] + y_in[p, 3, xl])
            yx_out[p, xl] = total

            @pl.when(2 * k + xl != x)
            def _(xl=xl):
                remote(yx_out.at[p, xl], yx_in.at[p, x], yx_s, yx_r.at[p], index(z, y, 2 * k + xl, k)).start()

    def gather(p):
        @pl.when(xh == k)
        def _():
            xy_in[p, y] = xy_out[p, y]
            yx_in[p, x] = yx_out[p, x & 1]
            received(3 * X // 16, xy_r.at[p])
            received(3 * Y // 16, yx_r.at[p])
            first = (xy_in[p, 0] + xy_in[p, 1]) + (xy_in[p, 2] + xy_in[p, 3])
            second = (yx_in[p, 0] + yx_in[p, 1]) + (yx_in[p, 2] + yx_in[p, 3])
            total = jnp.concatenate([first, second], axis=1)
            kp, q = p >> 1, p & 1
            zl = (q + x + y) & 1
            for zh in range(4):
                z_out[4 * p + zh] = total[2 * zh:2 * zh + 2]
                owner = index(2 * zh + zl, y, x, kp)

                @pl.when(owner == me)
                def _(zh=zh):
                    z_in[z] = total[2 * zh:2 * zh + 2]

                @pl.when(owner != me)
                def _(zh=zh, owner=owner):
                    remote(z_out.at[4 * p + zh], z_in.at[z], z_s, z_r, owner).start()

    @pl.when(k == 0)
    def _():
        sent(0)
        signal(mate)
        sent(1)

    @pl.when(k == 1)
    def _():
        pl.semaphore_wait(go, 1)
        send_all()

    def each(f, lo):
        def one(p, _):
            f(p)
            return 0

        lax.fori_loop(lo, lo + 2, one, 0)

    each(multiply, 0)
    each(combine, 0)
    each(middle, 0)

    def both(p):
        multiply(p)
        combine(p)

    @pl.when(k == 0)
    def _():
        each(both, 2)

    @pl.when(k == 1)
    def _():
        each(multiply, 2)
        each(combine, 2)

    each(gather, 0)
    each(middle, 2)
    each(gather, 2)

    for cond, count in ((xh == k, 7), (xh != k, 8)):
        @pl.when(cond)
        def _(count=count):
            got = z_in.at[pl.ds(0, count)]
            remote(got, got, z_s, z_r, mate).wait_recv()

    total = z_in[0]
    for s in range(1, 8):
        total = total + z_in[s]
    out[:, 0, :] = total[:, 0:800]
    out[:, 1, :] = total[:, 800:1600]

    @pl.when(k == 1)
    def _():
        sent(0)
        sent(1)

    remote(pair_in, pair_in, pair_s, pair_r.at[0, 0], mate).wait_send()
    departed(4 * 3 * Y // 8, y_s)
    for cond, count in ((xh == k, 1), (xh != k, 2)):
        @pl.when(cond)
        def _(count=count):
            departed(4 * count * X // 4, x_s)
            departed(4 * count * Y // 16, yx_s)

    @pl.when(xh == k)
    def _():
        departed(4 * 3 * X // 16, xy_s)

    @pl.when(xh == k)
    def _():
        part = z_out.at[pl.ds(0, 15)]
        remote(part, part, z_s, z_r, mate).wait_send()


def shards(amplitudes, integrals):
    tiles = amplitudes.reshape(2, 5000, LANES).transpose(1, 0, 2)
    dma = pltpu.SemaphoreType.DMA
    return pl.pallas_call(
        kernel,
        out_shape=jax.ShapeDtypeStruct((2, 2, 800), jnp.float32),
        in_specs=[pl.BlockSpec(memory_space=pl.ANY), pl.BlockSpec(memory_space=pl.ANY)],
        out_specs=pl.BlockSpec(memory_space=pltpu.VMEM),
        scratch_shapes=[
            pltpu.VMEM((PHASES, TILES, SOURCES, 2, LANES), jnp.bfloat16),
            pltpu.VMEM((8, 16, TILES + 1, 2, LANES), jnp.bfloat16),
            pltpu.VMEM((ROWS, WIDTH), jnp.bfloat16),
            pltpu.VMEM((TILES * LANES, WIDE), jnp.bfloat16),
            pltpu.VMEM((PHASES, 128, WIDE), jnp.float32),
            pltpu.VMEM((PHASES, 64, WIDE), jnp.float32),
            pltpu.VMEM((PHASES, 2, 4, 8, CUTS[0][1]), jnp.float32),
            pltpu.VMEM((PHASES, 4, 4, 8, CUTS[0][1]), jnp.float32),
            pltpu.VMEM((PHASES, 4, 8, CUTS[0][1]), jnp.float32),
            pltpu.VMEM((PHASES, 4, 8, CUTS[0][1]), jnp.float32),
            pltpu.VMEM((PHASES, 4, 2, 8, WIDE - CUTS[0][1]), jnp.float32),
            pltpu.VMEM((PHASES, 4, 2, 8, WIDE - CUTS[0][1]), jnp.float32),
            pltpu.VMEM((PHASES, 2, 8, WIDE - CUTS[0][1]), jnp.float32),
            pltpu.VMEM((PHASES, 4, 8, WIDE - CUTS[0][1]), jnp.float32),
            pltpu.VMEM((PHASES * 4, 2, WIDE), jnp.float32),
            pltpu.VMEM((8, 2, WIDE), jnp.float32),
            dma((2,)), dma((PHASES,)), pltpu.SemaphoreType.REGULAR, dma, dma, dma,
            dma, dma((PHASES, 2)), dma, dma((PHASES,)), dma, dma((PHASES,)), dma, dma((PHASES,)), dma, dma((PHASES,)), dma, dma,
        ],
        compiler_params=pltpu.CompilerParams(collective_id=1, has_side_effects=True, vmem_limit_bytes=60 << 20),
        name="ladder",
    )(tiles, integrals.reshape(ROWS, WIDTH))


def solution(mesh):
    return jax.shard_map(
        shards,
        mesh=mesh,
        in_specs=(P(("row", "col"), None), P(None, None, ("row", "col"))),
        out_specs=P(("row", "col"), None, None),
        check_vma=False,
    )
```
